512 devices in a mesh: ctx: 32 (over y, x), mem: 16 (over z, core).
Axes of the slice: x: 4, y: 8, z: 8, core: 2. Of those that a mesh axis runs over, the one named last changes fastest.
Arguments:
- queries: bfloat16 [65536, 1024], P(('ctx', 'mem')), may hold values from -6 to 6
- key_vectors: bfloat16 [65536, 1024], P(('ctx', 'mem')), may hold values from -30 to 30
- value_vectors: bfloat16 [65536, 1024], P(('ctx', 'mem')), may hold values from -30 to 30
- log_decay: bfloat16 [65536, 16], P(('ctx', 'mem')), may hold values from -1 to 0
- routes: int32 [65536, 2], P(('ctx', 'mem')), may hold values from 0 to 15, all different within a row; in each aligned block of 128 rows (0 to 127, 128 to 255, ...) at most 24 rows name the same one
- route_weight: float32 [65536, 2], P(('ctx', 'mem')), may hold values from 0.2 to 1
- out_gain: float32 [1024], replicated, may hold values from 0.5 to 1.5
Outputs:
- mixed_out: bfloat16 [65536, 1024], P(('ctx', 'mem'))
The draws below stay inside these ranges and needn't reach their ends.
Inputs may be any that keep to these rules, and one draw needn't show every extreme that they name: `routes`: each token names 2 different memories; among the 128 tokens of one device (aligned blocks) no memory is named more than 24 times, and in every draw some memory is named exactly 24 times.
All inputs are finite; a program needn't handle non-finite values.
Results may differ from the reference program's by a relative error of at most 0.0046.
Values may be sent and summed in bfloat16 or wider, within the bound.
No kernel may reach another device: no remote copies, remote signals or barrier semaphores. Data moves between devices by JAX's collectives and lax.ppermute only.
A program may use at most 128 MiB of HBM per device.

```python
import math
import jax
import jax.numpy as jnp
import numpy as np
from jax import lax

ATTN_SUBSET = 16
DH = 64
TOP = 2
TOK_DEV = 128
MEMS = 16
CAP = 24
SBLK = 256
SEQ_SPAN_COUNT = 65536
GROUP_TOK = 2048


def group_level(key):
    level_key = jax.random.fold_in(key, 911)
    pieces = jax.random.split(level_key, 3)
    group_count = SEQ_SPAN_COUNT // GROUP_TOK
    loud_group = jax.random.uniform(pieces[0], (group_count,)) < 0.34
    loud_level = jax.random.uniform(pieces[1], (group_count,), minval=1.4, maxval=2.0)
    quiet_level = jax.random.uniform(pieces[2], (group_count,), minval=-3.2, maxval=-2.6)
    level = jnp.exp(jnp.where(loud_group, loud_level, quiet_level))
    return jnp.repeat(level, GROUP_TOK)


def leveled_draw(key, salt):
    level = group_level(key)
    entry_key = jax.random.fold_in(key, salt)
    shape = (SEQ_SPAN_COUNT, ATTN_SUBSET * DH)
    base = jnp.clip(jax.random.normal(entry_key, shape), -4.0, 4.0)
    return (base * level[:, None]).astype(jnp.float32).astype(jnp.bfloat16)


def draw_key_vectors(key, part):
    return leveled_draw(key, 1)


def draw_value_vectors(key, part):
    return leveled_draw(key, 2)


def draw_log_decay(key, part):
    keys = jax.random.split(key, 8)
    fast_count = 3 * ATTN_SUBSET // 16
    middle_count = 5 * ATTN_SUBSET // 16
    head_order = jax.random.permutation(keys[0], ATTN_SUBSET)
    rapid_store = head_order < fast_count
    middle_store = (head_order >= fast_count) & (head_order < fast_count + middle_count)
    fast_len = jax.random.uniform(keys[1], (ATTN_SUBSET,), minval=30.0, maxval=50.0)
    keep = jax.random.uniform(keys[2], (ATTN_SUBSET,), minval=0.5, maxval=0.85)
    phase = jax.random.uniform(keys[3], (ATTN_SUBSET,), minval=0.0, maxval=6.283)
    store_slots_list = jax.random.randint(keys[4], (2,), 0, SEQ_SPAN_COUNT)
    objective_numbers = jax.random.uniform(keys[5], (2, ATTN_SUBSET), minval=0.5, maxval=0.8)
    group_fade = jax.random.uniform(keys[7], (ATTN_SUBSET,), minval=7.1, maxval=7.9)
    jitter = jnp.exp(0.15 * jnp.clip(jax.random.normal(keys[6], (SEQ_SPAN_COUNT, ATTN_SUBSET)), -2.0, 2.0))
    present_spot = jnp.arange(SEQ_SPAN_COUNT, dtype=jnp.int32)
    wave = jnp.exp(0.7 * jnp.sin(6.283 * 3.0 * present_spot[:, None].astype(jnp.float32) / SEQ_SPAN_COUNT + phase[None, :]))
    slow_forget_factor = jnp.log(keep)[None, :] / SEQ_SPAN_COUNT * wave * jitter
    rapid_forget_factor = -wave * jitter / fast_len[None, :]
    middle_forget_factor = -jitter * group_fade[None, :] / GROUP_TOK
    spike_extent = jnp.zeros((SEQ_SPAN_COUNT, ATTN_SUBSET), jnp.float32)
    for step_ordinal in range(2):
        spike_extent = spike_extent + jnp.where(present_spot[:, None] == store_slots_list[step_ordinal], jnp.log(objective_numbers[step_ordinal])[None, :], 0.0)
    forget_factor = jnp.where(rapid_store[None, :], rapid_forget_factor, jnp.where(middle_store[None, :], middle_forget_factor, slow_forget_factor + spike_extent))
    forget_factor = jnp.clip(forget_factor, -1.0, 0.0)
    return forget_factor.astype(jnp.float32).astype(jnp.bfloat16)


def block_levels(rng, dims, cuts, least, largest):
    def one(dim, parts):
        steps = jax.random.uniform(jax.random.fold_in(jax.random.fold_in(rng, 6), dim), (parts,), jnp.float32, least / len(cuts), largest / len(cuts))
        return jnp.repeat(jnp.exp(steps), dims[dim] // parts).reshape((-1,) + (1,) * (len(dims) - dim - 1))

    loudness = one(*cuts[0])
    for cut in cuts[1:]:
        loudness = loudness * one(*cut)
    return loudness


def routed_block(key, own, number, rows, count, top, bound, slope):
    order = jax.random.permutation(key, count)
    packed, common = load_shares(count, rows * top, bound, slope, True), load_shares(count, rows * top, bound, slope, False)
    places = jnp.arange(count)

    def named(tallies, offset_by):
        used = int((tallies > 0).sum())
        fixed = max(1, used // 4)
        shifted = fixed + (places - fixed + offset_by * (used - fixed)) % max(1, count - fixed)
        return jnp.zeros((count,), jnp.int32).at[order[jnp.where(places < fixed, places, shifted)]].set(jnp.asarray(tallies, jnp.int32))

    tallies = jnp.where(number % 4 == 0, named(packed, number // 4), named(common, number - number // 4 - 1))
    mixed = jax.random.permutation(jax.random.fold_in(own, 3), count)
    source_of, receiver = mixed[0:count // 2 * 2:2], mixed[1:count // 2 * 2:2]
    margin = jnp.minimum(tallies[source_of] - 1, bound - tallies[receiver]) // 2
    margin = jnp.where((source_of == order[0]) | (receiver == order[0]) | (tallies[receiver] == 0), 0, jnp.maximum(margin, 0))
    shifted = jax.random.randint(jax.random.fold_in(own, 4), (count // 2,), 0, 1 << 20) % (margin + 1)
    tallies = tallies.at[source_of].add(-shifted).at[receiver].add(shifted)
    members = jnp.searchsorted(jnp.cumsum(tallies), jnp.arange(rows * top), side="right").astype(jnp.int32)
    grid = members.reshape(top, rows).T
    grid = grid[jax.random.permutation(jax.random.fold_in(own, 1), rows)]
    offset_by = jax.random.randint(jax.random.fold_in(own, 2), (rows, 1), 0, top)
    return jnp.take_along_axis(grid, (jnp.arange(top)[None, :] + offset_by) % top, axis=1)


def load_shares(number_of, total, most, lean, full):
    portions = [(1 << 20) // math.isqrt(rank ** lean) + 1 for rank in range(1, number_of + 1)]
    largest = most if full else min(most, max(-(-total // number_of), total * portions[0] // sum(portions)))
    least = 1 if total - largest >= number_of - 1 else 0
    given, surplus = [largest] + [least] * (number_of - 1), total - largest - least * (number_of - 1)
    while surplus > 0:
        candidates = [i for i in range(1, number_of) if given[i] < largest] or [i for i in range(1, number_of) if given[i] < most]
        mass, budget = sum([portions[i] for i in candidates]), surplus
        for i in candidates:
            more = min(most - given[i], max(1, budget * portions[i] // mass), surplus)
            given[i] = given[i] + more
            surplus = surplus - more
    return np.array(given)


def bell_draw(key, dims, width, reach, cuts=(), kind=jnp.bfloat16):
    values = width * jax.random.normal(key, dims, jnp.float32)
    if cuts:
        values = values * block_levels(key, dims, cuts, -0.22, 0.18)
    return jnp.clip(values, -reach, reach).astype(kind)


def setup_inputs(seed: int = 0) -> dict:
    streams_of = jax.random.split(jax.random.key(seed), 8)
    queries = bell_draw(streams_of[0], (SEQ_SPAN_COUNT, ATTN_SUBSET * DH), 1.0, 6.0, ((0, 512),))
    key_vectors = draw_key_vectors(jax.random.fold_in(streams_of[7], 71), 0)
    value_vectors = draw_value_vectors(jax.random.fold_in(streams_of[7], 71), 0)
    log_decay = draw_log_decay(jax.random.fold_in(streams_of[7], 71), 0)
    routes_keys = jax.random.split(jax.random.fold_in(streams_of[4], 1), SEQ_SPAN_COUNT // TOK_DEV)
    routes_turns = jax.random.permutation(jax.random.fold_in(streams_of[4], 3), SEQ_SPAN_COUNT // TOK_DEV)
    routes = jax.vmap(lambda own, number: routed_block(jax.random.fold_in(streams_of[4], 2), own, number, TOK_DEV, MEMS, TOP, CAP, 2))(routes_keys, routes_turns).reshape((SEQ_SPAN_COUNT, TOP))
    route_weight = jnp.clip(0.2 + 0.8 * jax.random.uniform(streams_of[5], (SEQ_SPAN_COUNT, TOP), jnp.float32) ** block_levels(streams_of[5], (SEQ_SPAN_COUNT, TOP), ((0, 512),), -0.2, 0.2), 0.2, 1.0)
    out_gain = jnp.clip(1.0 + 0.1 * jax.random.normal(streams_of[6], (ATTN_SUBSET * DH,), jnp.float32), 0.5, 1.5)
    return {"queries": queries, "key_vectors": key_vectors, "value_vectors": value_vectors, "log_decay": log_decay, "routes": routes, "route_weight": route_weight, "out_gain": out_gain}


precise = lax.Precision.HIGHEST

def block_run(query_blk, key_blk, value_blk, decay_blk):
    head_count = query_blk.shape[2]
    head_size = query_blk.shape[3]

    def advance(state, pieces):
        query_now, key_now, value_now, decay_now = pieces
        cumul = jnp.cumsum(decay_now, axis=0)
        store_slots_list = jnp.arange(query_now.shape[0], dtype=jnp.int32)
        causal = (store_slots_list[:, None] >= store_slots_list[None, :])[None]
        spread = jnp.transpose(cumul)[:, :, None] - jnp.transpose(cumul)[:, None, :]
        factor = jnp.where(causal, jnp.exp(jnp.where(causal, spread, 0.0)), 0.0)
        query_wide = query_now.astype(jnp.float32)
        value_wide = value_now.astype(jnp.float32)
        scores = jnp.einsum('lhd,shd->hls', query_wide, key_now.astype(jnp.float32))
        weights = lax.optimization_barrier((scores * factor).astype(jnp.bfloat16)).astype(jnp.float32)
        inner = jnp.einsum('hls,shd->lhd', weights, value_wide)
        outer = jnp.einsum('lhd,hde->lhe', query_wide * jnp.exp(cumul)[:, :, None], state, precision=precise)
        last = cumul[-1]
        faded = key_now.astype(jnp.float32) * jnp.exp(last[None, :] - cumul)[:, :, None]
        state = jnp.exp(last)[:, None, None] * state + jnp.einsum('lhd,lhe->hde', faded, value_wide, precision=precise)
        return (state, inner + outer)
    start = jnp.zeros((head_count, head_size, head_size), jnp.float32)
    final_state, outputs = lax.scan(advance, start, (query_blk, key_blk, value_blk, decay_blk))
    return outputs

def reference(queries, key_vectors, value_vectors, log_decay, routes, route_weight, out_gain):
    tok_total = queries.shape[0]
    query_heads = queries.reshape(tok_total, ATTN_SUBSET, DH)
    key_heads = key_vectors.reshape(tok_total, ATTN_SUBSET, DH)
    value_heads = value_vectors.reshape(tok_total, ATTN_SUBSET, DH)
    decay = log_decay.astype(jnp.float32)
    block_count = tok_total // SBLK
    shared = block_run(query_heads.reshape(block_count, SBLK, ATTN_SUBSET, DH), key_heads.reshape(block_count, SBLK, ATTN_SUBSET, DH), value_heads.reshape(block_count, SBLK, ATTN_SUBSET, DH), decay.reshape(block_count, SBLK, ATTN_SUBSET))
    shared = lax.optimization_barrier(shared.reshape(tok_total, ATTN_SUBSET, DH).astype(jnp.bfloat16)).astype(jnp.float32)
    dev_count = tok_total // TOK_DEV
    mem_ids = jnp.arange(MEMS, dtype=jnp.int32)
    member = routes[:, :, None] == mem_ids[None, None, :]
    assign = lax.optimization_barrier(jnp.sum(member.astype(jnp.int32), axis=1)).astype(jnp.int32)
    blocked = assign.reshape(dev_count, TOK_DEV, MEMS)
    ranked = (jnp.cumsum(blocked, axis=1).astype(jnp.int32) - blocked).reshape(tok_total, MEMS)
    owner_dev = (jnp.arange(tok_total, dtype=jnp.int32) // TOK_DEV).astype(jnp.int32)
    position = (owner_dev[:, None] * CAP + ranked).astype(jnp.int32)
    slot_total = dev_count * CAP
    span = SBLK // TOK_DEV * CAP

    def per_memory(total, memory):
        chosen = assign[:, memory] == 1
        where_to = jnp.where(chosen, position[:, memory], slot_total).astype(jnp.int32)

        def placed(array):
            empty = jnp.zeros((slot_total,) + array.shape[1:], array.dtype)
            return empty.at[where_to].set(array, mode='drop')
        slot_q = placed(query_heads).reshape(slot_total // span, span, ATTN_SUBSET, DH)
        slot_k = placed(key_heads).reshape(slot_total // span, span, ATTN_SUBSET, DH)
        slot_v = placed(value_heads).reshape(slot_total // span, span, ATTN_SUBSET, DH)
        slot_g = placed(decay).reshape(slot_total // span, span, ATTN_SUBSET)
        routed = block_run(slot_q, slot_k, slot_v, slot_g).reshape(slot_total, ATTN_SUBSET, DH)
        routed = lax.optimization_barrier(routed.astype(jnp.bfloat16)).astype(jnp.float32)
        picked = routed[jnp.minimum(where_to, slot_total - 1)]
        share = lax.optimization_barrier(jnp.sum(jnp.where(member[:, :, memory], route_weight, 0.0), axis=1))
        return (total + share[:, None, None] * picked, None)
    routed_sum, leftover = lax.scan(per_memory, jnp.zeros((tok_total, ATTN_SUBSET, DH), jnp.float32), mem_ids)
    combined = shared + routed_sum
    scale = lax.rsqrt(lax.optimization_barrier(jnp.mean(combined * combined, axis=-1, keepdims=True)) + 1e-06)
    result = combined * scale * out_gain.reshape(ATTN_SUBSET, DH)
    return result.astype(jnp.bfloat16).reshape(tok_total, ATTN_SUBSET * DH)
```

```python
import functools

import jax
import jax.numpy as jnp
from jax import lax
from jax.experimental import pallas as pl
from jax.experimental.pallas import tpu as pltpu
from jax.sharding import PartitionSpec as P

MEMS = 16
SETS = 17
ROWS = 24
EXTRA = 16
BF = jnp.bfloat16
F32 = jnp.float32


def iota(shape, dim):
    return lax.broadcasted_iota(jnp.int32, shape, dim)


def dot(a, b, ca, cb):
    return lax.dot_general(a, b, (((ca,), (cb,)), ((), ())), preferred_element_type=F32)


def halves(x):
    high = x.astype(BF)
    return high, (x - high.astype(F32)).astype(BF)


def call(body, out_shape, *args, scratch=(), name=None):
    return pl.pallas_call(
        body,
        out_shape=out_shape,
        scratch_shapes=list(scratch),
        name=name,
        compiler_params=pltpu.CompilerParams(vmem_limit_bytes=48 << 20),
    )(*args)


def spread_body(k_ref, v_ref, g_ref, r_ref, w_ref, out_ref):
    width = k_ref.shape[0]
    head_size = k_ref.shape[1] // out_ref.shape[0]
    per = 128 // head_size
    eye = (iota((128, 128), 0) == iota((128, 128), 1)).astype(BF)
    routes = r_ref[...].astype(F32)
    weights = w_ref[...]
    high = weights.astype(BF).astype(F32)
    low = weights - high
    rows = iota((EXTRA, width), 0)
    common = jnp.zeros((EXTRA, width), F32)
    for place, line in enumerate(
        (routes[0:1], routes[1:2], high[0:1], high[1:2], low[0:1], low[1:2])
    ):
        common = jnp.where(rows == place + 1, line, common)
    decay = g_ref[...].astype(F32)
    for chunk in range(k_ref.shape[1] // 128):
        for base, ref in ((0, k_ref), (head_size, v_ref)):
            turned = dot(eye, ref[:, chunk * 128 : (chunk + 1) * 128], 1, 1).astype(BF)
            for part in range(per):
                out_ref[chunk * per + part, base : base + head_size, :] = turned[
                    part * head_size : (part + 1) * head_size, :
                ]
    for head in range(out_ref.shape[0]):
        out_ref[head, 2 * head_size : 2 * head_size + EXTRA, :] = jnp.where(
            rows == 0, decay[head : head + 1], common
        ).astype(BF)


def turn_body(q_ref, out_ref):
    head_size = out_ref.shape[1]
    per = 128 // head_size
    eye = (iota((128, 128), 0) == iota((128, 128), 1)).astype(BF)
    for chunk in range(q_ref.shape[1] // 128):
        turned = dot(eye, q_ref[:, chunk * 128 : (chunk + 1) * 128], 1, 1).astype(BF)
        for part in range(per):
            out_ref[chunk * per + part] = turned[part * head_size : (part + 1) * head_size, :]


def back_body(x_ref, out_ref):
    head_size = x_ref.shape[1]
    per = 128 // head_size
    eye = (iota((128, 128), 0) == iota((128, 128), 1)).astype(BF)
    for chunk in range(out_ref.shape[1] // 128):
        slab = x_ref[chunk * per : (chunk + 1) * per].reshape(128, 128)
        out_ref[:, chunk * 128 : (chunk + 1) * 128] = dot(eye, slab, 1, 1).astype(BF)


def tables(extra):
    width = extra.shape[1]
    ids = iota((ROWS, width), 0).astype(F32)
    first, second = extra[1:2], extra[2:3]
    member = (ids == first) | (ids == second) | (ids == float(MEMS))
    upper = (iota((width, width), 0) <= iota((width, width), 1)).astype(BF)
    decay = jnp.where(member, extra[0:1], 0.0).astype(BF)
    cumul = dot(decay, upper, 1, 0)
    return member, cumul, cumul[:, width - 1 : width]


def read_weights(extra):
    width = extra.shape[1]
    ids = iota((ROWS, width), 0).astype(F32)
    zero = jnp.zeros((ROWS, width), F32)
    return (
        jnp.where(ids == extra[1:2], extra[3:4] + extra[5:6], zero)
        + jnp.where(ids == extra[2:3], extra[4:5] + extra[6:7], zero)
        + jnp.where(ids == float(MEMS), 1.0, zero)
    )


def added(kv_ref, block, reach, scale, out):
    head_size = (kv_ref.shape[1] - EXTRA) // 2
    keys = kv_ref[block, 0:head_size, :]
    values = kv_ref[block, head_size : 2 * head_size, :].astype(F32)
    twice = jnp.concatenate([keys, keys], axis=0)
    twice = jnp.concatenate([twice, twice], axis=1)
    for one in range(SETS):
        high, low = halves(values * reach[one : one + 1])
        fresh = dot(jnp.concatenate([high, low], axis=1), twice, 1, 1)
        out(one, fresh)


def totals_body(pieces, kv_ref, out_ref, state_ref):
    blocks, height, width = kv_ref.shape
    head_size = (height - EXTRA) // 2
    state_ref[...] = jnp.zeros_like(state_ref)

    def step(turn, after):
        block = blocks - 1 - turn
        extra = kv_ref[block, 2 * head_size : height, :].astype(F32)
        member, cumul, total = tables(extra)
        reach = jnp.where(member, jnp.exp(total - cumul + after), 0.0)

        def out(one, fresh):
            state_ref[one] += fresh

        added(kv_ref, block, reach, None, out)
        return after + total

    after = lax.fori_loop(0, blocks, step, jnp.zeros((ROWS, width), F32))
    left = iota((8, width), 1) < head_size
    rows = iota((8, width), 0)
    parts = pieces // MEMS
    lines = head_size // 2 // parts
    plain = after.astype(BF).astype(F32)
    middle = (after - plain).astype(BF).astype(F32)
    rest = after - plain - middle
    for piece in range(pieces):
        one, part = piece // parts, piece % parts
        for base in range(0, lines, 8):
            start = part * 2 * lines + base
            out_ref[piece, base : base + 8, :] = jnp.where(
                left,
                state_ref[one, start : start + 8, :],
                state_ref[one, start + lines : start + lines + 8, :],
            ).astype(out_ref.dtype)
        shared = jnp.where(
            left[0:1],
            state_ref[MEMS, piece : piece + 1, :],
            state_ref[MEMS, piece + head_size // 2 : piece + head_size // 2 + 1, :],
        )
        tail = jnp.where(rows == 0, shared, 0.0)
        for place, line in enumerate(
            (plain[one : one + 1], middle[one : one + 1], rest[one : one + 1],
             plain[MEMS : MEMS + 1], middle[MEMS : MEMS + 1], rest[MEMS : MEMS + 1])
        ):
            tail = jnp.where(rows == place + 1, line, tail)
        out_ref[piece, lines : lines + 8, :] = tail.astype(out_ref.dtype)


def prefix_body(x_ref, out_ref):
    peers, height, width = x_ref.shape
    lines = height - 8
    rows = iota((height, width), 0)
    before = jnp.zeros((height, width), F32)
    for peer in range(peers):
        out_ref[peer] = before.astype(out_ref.dtype)
        if peer < peers - 1:
            own = x_ref[peer].astype(F32)
            routed = own[lines + 1 : lines + 2] + own[lines + 2 : lines + 3] + own[lines + 3 : lines + 4]
            shared = own[lines + 4 : lines + 5] + own[lines + 5 : lines + 6] + own[lines + 6 : lines + 7]
            fade = jnp.exp(jnp.where(rows < lines, routed, shared))
            before = fade * before + own


def local_body(kv_ref, q_ref, out_ref, lift_ref, state_ref):
    blocks, height, width = kv_ref.shape
    head_size = (height - EXTRA) // 2
    state_ref[...] = jnp.zeros_like(state_ref)

    def step(block, offset):
        extra = kv_ref[block, 2 * head_size : height, :].astype(F32)
        member, cumul, total = tables(extra)
        share = read_weights(extra)
        lift_ref[block] = share * jnp.exp(cumul + offset)
        keys = kv_ref[block, 0:head_size, :]
        values = kv_ref[block, head_size : 2 * head_size, :]
        queries = q_ref[block]
        middle = cumul[:, width // 2 - 1 : width // 2]
        write_high, write_low = halves(jnp.where(member, jnp.exp(middle - cumul), 0.0))
        read_high, read_low = halves(share * jnp.exp(cumul - middle))
        factor = dot(
            jnp.concatenate([write_high, write_low, write_high], axis=0),
            jnp.concatenate([read_high, read_high, read_low], axis=0),
            0,
            0,
        )
        causal = iota((width, width), 0) <= iota((width, width), 1)
        scores = dot(keys, queries, 0, 0)
        high, low = halves(jnp.where(causal, scores * factor, 0.0))
        total_out = dot(
            jnp.concatenate([values, values], axis=1), jnp.concatenate([high, low], axis=0), 1, 0
        )
        pair = jnp.concatenate([queries, queries], axis=0)
        lift = share * jnp.exp(cumul)
        left = iota((head_size, 2 * head_size), 1) < head_size
        fade = jnp.exp(total)
        for one in range(SETS):
            high, low = halves(state_ref[one])
            seen = dot(jnp.where(left, high, low), pair, 1, 0)
            total_out = total_out + lift[one : one + 1] * seen
        out_ref[block] = total_out
        reach = jnp.where(member, jnp.exp(total - cumul), 0.0)

        def out(one, fresh):
            state_ref[one] = fade[one : one + 1] * state_ref[one] + fresh

        added(kv_ref, block, reach, fade, out)
        return offset + total

    lax.fori_loop(0, blocks, step, jnp.zeros((ROWS, width), F32))


def finish_body(before_ref, q_ref, local_ref, lift_ref, gain_ref, out_ref, shared_ref):
    pieces = before_ref.shape[0]
    lines = before_ref.shape[1] - 8
    blocks, head_size, width = q_ref.shape
    parts = pieces // MEMS
    half = head_size // 2
    for piece in range(pieces):
        shared_ref[piece : piece + 1, :] = before_ref[piece, lines : lines + 8, :].astype(F32)[0:1]
    gain = gain_ref[...]

    def step(block, carry):
        queries = q_ref[block]
        zero = jnp.zeros_like(queries)
        sides = jnp.concatenate(
            [jnp.concatenate([queries, zero], axis=1), jnp.concatenate([zero, queries], axis=1)],
            axis=0,
        )
        lift = lift_ref[block]
        both = dot(shared_ref[...].astype(BF), sides, 1, 0)
        line = lift[MEMS : MEMS + 1]
        add = jnp.concatenate([both[:, :width], both[:, width:]], axis=0) * line
        groups = [add[2 * lines * part : 2 * lines * (part + 1)] for part in range(parts)]
        for piece in range(pieces):
            one, part = piece // parts, piece % parts
            seen = dot(before_ref[piece, 0:lines, :].astype(BF), sides, 1, 0)
            line = lift[one : one + 1]
            groups[part] = groups[part] + line * jnp.concatenate(
                [seen[:, :width], seen[:, width:]], axis=0
            )
        combined = local_ref[block] + jnp.concatenate(groups, axis=0)
        mean = jnp.sum(combined * combined, axis=0, keepdims=True) * (1.0 / head_size)
        out_ref[block] = (combined * lax.rsqrt(mean + 1e-06) * gain).astype(BF)
        return carry

    lax.fori_loop(0, blocks, step, 0)


def shape(dims, dtype):
    return jax.ShapeDtypeStruct(dims, dtype)


def exchange(x, axis):
    return lax.all_to_all(x, axis, split_axis=0, concat_axis=0, tiled=True)


SEND = BF


def spread(keys, values, decay, routes, weights, heads):
    width = keys.shape[0]
    head_size = keys.shape[1] // heads
    return call(
        spread_body, shape((heads, 2 * head_size + EXTRA, width), BF),
        keys, values, decay.T, routes.T, weights.T, name="spread",
    )


def turn(queries, heads):
    return call(
        turn_body, shape((heads, queries.shape[1] // heads, queries.shape[0]), BF), queries,
        name="turn",
    )


def totals(kv, pieces):
    head_size, width = (kv.shape[1] - EXTRA) // 2, kv.shape[2]
    lines = MEMS * head_size // 2 // pieces
    return call(
        functools.partial(totals_body, pieces), shape((pieces, lines + 8, width), SEND), kv,
        scratch=[pltpu.VMEM((SETS, head_size, width), F32)], name="totals",
    )


def prefix(x):
    return call(prefix_body, shape(x.shape, x.dtype), x, name="prefix")


def local(kv, q):
    blocks, head_size, width = q.shape
    return call(
        local_body,
        (shape((blocks, head_size, width), F32), shape((blocks, ROWS, width), F32)),
        kv, q, scratch=[pltpu.VMEM((SETS, head_size, width), F32)], name="local",
    )


def finish(before, q, inner, lift, gain):
    head_size, width = q.shape[1:]
    return call(
        finish_body, shape(q.shape, BF), before, q, inner, lift, gain,
        scratch=[pltpu.VMEM((head_size // 2, width), F32)], name="finish",
    )


def back(x, tokens, feats):
    return call(back_body, shape((tokens, feats), BF), x, name="back")


def on_device(queries, key_vectors, value_vectors, log_decay, routes, route_weight, out_gain):
    heads = lax.axis_size("mem")
    pieces = lax.axis_size("ctx")
    tokens, feats = queries.shape
    head_size = feats // heads
    kv = exchange(spread(key_vectors, value_vectors, log_decay, routes, route_weight, heads), "mem")
    q = exchange(turn(queries, heads), "mem")
    gathered = exchange(totals(kv, pieces), "ctx")
    inner, lift = local(kv, q)
    before = exchange(prefix(gathered), "ctx")
    mine = lax.dynamic_slice_in_dim(out_gain, lax.axis_index("mem") * head_size, head_size)
    gain = jnp.broadcast_to(mine[:, None], (head_size, tokens))
    done = exchange(finish(before, q, inner, lift, gain), "mem")
    return back(done, tokens, feats)


def solution(mesh):
    rows = P(("ctx", "mem"), None)
    return jax.shard_map(
        on_device,
        mesh=mesh,
        in_specs=(rows, rows, rows, rows, rows, rows, P()),
        out_specs=rows,
        check_vma=False,
    )
```

```python
import functools

import jax
import jax.numpy as jnp
from jax import lax
from jax.experimental import pallas as pl
from jax.experimental.pallas import tpu as pltpu
from jax.sharding import PartitionSpec as P


MEMS = 16
SETS = 17
ROWS = 24
EXTRA = 16
BF = jnp.bfloat16
F32 = jnp.float32


def iota(shape, dim):
    return lax.broadcasted_iota(jnp.int32, shape, dim)


def dot(a, b, ca, cb):
    return lax.dot_general(a, b, (((ca,), (cb,)), ((), ())), preferred_element_type=F32)


def halves(x):
    high = x.astype(BF)
    return high, (x - high.astype(F32)).astype(BF)


def call(body, out_shape, *args, scratch=(), fetch=False):
    specs = {"in_specs": [pl.BlockSpec(memory_space=pltpu.HBM)] * len(args)} if fetch else {}
    return pl.pallas_call(
        body,
        out_shape=out_shape,
        **specs,
        scratch_shapes=list(scratch),
        compiler_params=pltpu.CompilerParams(vmem_limit_bytes=48 << 20),
    )(*args)


def fetched(body, count):
    def kernel(*refs):
        given, out_ref, held, sems = refs[:count], refs[count], refs[count + 1 : -1], refs[-1]
        copies = [
            pltpu.make_async_copy(source, target, sems.at[place])
            for place, (source, target) in enumerate(zip(given, held))
        ]
        for copy in copies:
            copy.start()
        for copy in copies:
            copy.wait()
        body(*held, out_ref)

    return kernel


def held(args):
    return [pltpu.VMEM(a.shape, a.dtype) for a in args] + [pltpu.SemaphoreType.DMA((len(args),))]


def spread_body(k_ref, v_ref, g_ref, r_ref, w_ref, out_ref):
    width = k_ref.shape[0]
    head_size = k_ref.shape[1] // out_ref.shape[0]
    per = 128 // head_size
    eye = (iota((128, 128), 0) == iota((128, 128), 1)).astype(BF)
    routes = r_ref[...].astype(F32)
    weights = w_ref[...]
    high = weights.astype(BF).astype(F32)
    low = weights - high
    rows = iota((EXTRA, width), 0)
    common = jnp.zeros((EXTRA, width), F32)
    for place, line in enumerate(
        (routes[0:1], routes[1:2], high[0:1], high[1:2], low[0:1], low[1:2])
    ):
        common = jnp.where(rows == place + 1, line, common)
    decay = g_ref[...].astype(F32)
    for chunk in range(k_ref.shape[1] // 128):
        for base, ref in ((0, k_ref), (head_size, v_ref)):
            turned = dot(eye, ref[:, chunk * 128 : (chunk + 1) * 128], 1, 1).astype(BF)
            for part in range(per):
                out_ref[chunk * per + part, base : base + head_size, :] = turned[
                    part * head_size : (part + 1) * head_size, :
                ]
    for head in range(out_ref.shape[0]):
        out_ref[head, 2 * head_size : 2 * head_size + EXTRA, :] = jnp.where(
            rows == 0, decay[head : head + 1], common
        ).astype(BF)


def turn_body(q_ref, out_ref):
    head_size = out_ref.shape[1]
    per = 128 // head_size
    eye = (iota((128, 128), 0) == iota((128, 128), 1)).astype(BF)
    for chunk in range(q_ref.shape[1] // 128):
        turned = dot(eye, q_ref[:, chunk * 128 : (chunk + 1) * 128], 1, 1).astype(BF)
        for part in range(per):
            out_ref[chunk * per + part] = turned[part * head_size : (part + 1) * head_size, :]


def back_body(x_ref, out_ref):
    head_size = x_ref.shape[1]
    per = 128 // head_size
    eye = (iota((128, 128), 0) == iota((128, 128), 1)).astype(BF)
    for chunk in range(out_ref.shape[1] // 128):
        slab = x_ref[chunk * per : (chunk + 1) * per].reshape(128, 128)
        out_ref[:, chunk * 128 : (chunk + 1) * 128] = dot(eye, slab, 1, 1).astype(BF)


def tables(kv_ref):
    blocks, height, width = kv_ref.shape
    extra = kv_ref[:, height - EXTRA : height, :].astype(F32)
    ids = iota((blocks, ROWS, width), 1).astype(F32)
    member = (ids == extra[:, 1:2]) | (ids == extra[:, 2:3]) | (ids == float(MEMS))
    upper = (iota((width, width), 0) <= iota((width, width), 1)).astype(BF)
    decay = jnp.where(member, extra[:, 0:1], 0.0).reshape(blocks * ROWS, width).astype(BF)
    cumul = dot(decay, upper, 1, 0).reshape(blocks, ROWS, width)
    total = jnp.broadcast_to(cumul[:, :, width - 1 : width], cumul.shape)
    return extra, ids, member, cumul, total


def spread_out(kv_ref, block, reach, wide_ref, at):
    head_size = (kv_ref.shape[1] - EXTRA) // 2
    width = kv_ref.shape[2]
    keys = kv_ref[block, 0:head_size, :]
    values = kv_ref[block, head_size : 2 * head_size, :].astype(F32)
    for one in range(SETS):
        high, low = halves(values * reach[one : one + 1])
        rows = slice(one * head_size, (one + 1) * head_size)
        wide_ref[rows, at : at + width] = high
        wide_ref[rows, at + width : at + 2 * width] = low
    twice = jnp.concatenate([keys, keys], axis=0)
    return jnp.concatenate([twice, twice], axis=1)


TOGETHER = 2


def totals_body(pieces, kv_ref, out_ref, state_ref, reach_ref, wide_ref):
    blocks, height, width = kv_ref.shape
    head_size = (height - EXTRA) // 2
    _, _, member, cumul, total = tables(kv_ref)
    after = jnp.zeros((ROWS, width), F32)
    for block in reversed(range(blocks)):
        reach_ref[block] = jnp.where(
            member[block], jnp.exp(total[block] - cumul[block] + after), 0.0
        )
        after = after + total[block]
    state_ref[...] = jnp.zeros_like(state_ref)

    def step(turn, carry):
        keys = []
        for extra_block in range(TOGETHER):
            block = turn * TOGETHER + extra_block
            keys.append(
                spread_out(kv_ref, block, reach_ref[block], wide_ref, extra_block * 2 * width)
            )
        state_ref[...] += dot(wide_ref[...], jnp.concatenate(keys, axis=1), 1, 1)
        return carry

    lax.fori_loop(0, blocks // TOGETHER, step, 0)
    left = iota((8, width), 1) < head_size
    rows = iota((8, width), 0)
    parts = pieces // MEMS
    lines = head_size // 2 // parts
    plain = after.astype(BF).astype(F32)
    middle = (after - plain).astype(BF).astype(F32)
    rest = after - plain - middle
    for piece in range(pieces):
        one, part = piece // parts, piece % parts
        for base in range(0, lines, 8):
            start = one * head_size + part * 2 * lines + base
            out_ref[piece, base : base + 8, :] = jnp.where(
                left, state_ref[start : start + 8, :], state_ref[start + lines : start + lines + 8, :]
            ).astype(out_ref.dtype)
        start = MEMS * head_size + piece
        shared = jnp.where(
            left[0:1],
            state_ref[start : start + 1, :],
            state_ref[start + head_size // 2 : start + head_size // 2 + 1, :],
        )
        tail = jnp.where(rows == 0, shared, 0.0)
        for place, line in enumerate(
            (plain[one : one + 1], middle[one : one + 1], rest[one : one + 1],
             plain[MEMS : MEMS + 1], middle[MEMS : MEMS + 1], rest[MEMS : MEMS + 1])
        ):
            tail = jnp.where(rows == place + 1, line, tail)
        out_ref[piece, lines : lines + 8, :] = tail.astype(out_ref.dtype)


def prefix_body(x_ref, out_ref):
    peers, height, width = x_ref.shape
    lines = height - 8
    rows = iota((height, width), 0)
    before = jnp.zeros((height, width), F32)
    for peer in range(peers):
        out_ref[peer] = before.astype(out_ref.dtype)
        if peer < peers - 1:
            own = x_ref[peer].astype(F32)
            routed = own[lines + 1 : lines + 2] + own[lines + 2 : lines + 3] + own[lines + 3 : lines + 4]
            shared = own[lines + 4 : lines + 5] + own[lines + 5 : lines + 6] + own[lines + 6 : lines + 7]
            fade = jnp.exp(jnp.where(rows < lines, routed, shared))
            before = fade * before + own


def local_body(kv_ref, q_ref, out_ref, lift_ref, state_ref, pair_ref, wide_ref, reach_ref,
               read_ref, write_ref, fade_ref, near_ref):
    blocks, height, width = kv_ref.shape
    head_size = (height - EXTRA) // 2
    extra, ids, member, cumul, total = tables(kv_ref)
    share = (
        jnp.where(ids == extra[:, 1:2], extra[:, 3:4] + extra[:, 5:6], 0.0)
        + jnp.where(ids == extra[:, 2:3], extra[:, 4:5] + extra[:, 6:7], 0.0)
        + jnp.where(ids == float(MEMS), 1.0, 0.0)
    )
    middle = cumul[:, :, width // 2 - 1 : width // 2]
    write_ref[...] = jnp.where(member, jnp.exp(middle - cumul), 0.0)
    read_ref[...] = share * jnp.exp(cumul - middle)
    reach_ref[...] = jnp.where(member, jnp.exp(total - cumul), 0.0)
    fade_ref[...] = jnp.exp(total)
    near_ref[...] = share * jnp.exp(cumul)
    offset = jnp.zeros((ROWS, width), F32)
    for block in range(blocks):
        lift_ref[block] = share[block] * jnp.exp(cumul[block] + offset)
        offset = offset + total[block]
    state_ref[...] = jnp.zeros_like(state_ref)
    pair_ref[...] = jnp.zeros_like(pair_ref)

    def step(block, carry):
        keys = kv_ref[block, 0:head_size, :]
        values = kv_ref[block, head_size : 2 * head_size, :]
        queries = q_ref[block]
        pair = jnp.concatenate([queries, queries], axis=0)
        seen = dot(pair_ref[...], pair, 1, 0)
        write_high, write_low = halves(write_ref[block])
        read_high, read_low = halves(read_ref[block])
        factor = dot(
            jnp.concatenate([write_high, write_low, write_high], axis=0),
            jnp.concatenate([read_high, read_high, read_low], axis=0),
            0,
            0,
        )
        causal = iota((width, width), 0) <= iota((width, width), 1)
        scores = dot(keys, queries, 0, 0)
        high, low = halves(jnp.where(causal, scores * factor, 0.0))
        result = dot(
            jnp.concatenate([values, values], axis=1), jnp.concatenate([high, low], axis=0), 1, 0
        )
        lift = near_ref[block]
        fade = fade_ref[block]
        twice = spread_out(kv_ref, block, reach_ref[block], wide_ref, 0)
        fresh = dot(wide_ref[...], twice, 1, 1)
        left = iota((head_size, 2 * head_size), 1) < head_size
        for one in range(SETS):
            rows = slice(one * head_size, (one + 1) * head_size)
            result = result + lift[one : one + 1] * seen[rows]
            state = fade[one : one + 1] * state_ref[rows] + fresh[rows]
            state_ref[rows] = state
            high, low = halves(state)
            pair_ref[rows] = jnp.where(left, high, low)
        out_ref[block] = result
        return carry

    lax.fori_loop(0, blocks, step, 0)


def finish_body(before_ref, q_ref, local_ref, lift_ref, gain_ref, out_ref, all_ref, shared_ref):
    pieces = before_ref.shape[0]
    lines = before_ref.shape[1] - 8
    blocks, head_size, width = q_ref.shape
    parts = pieces // MEMS
    half = head_size // 2
    for piece in range(pieces):
        all_ref[piece * lines : (piece + 1) * lines, :] = before_ref[piece, 0:lines, :]
        shared_ref[piece : piece + 1, :] = before_ref[piece, lines : lines + 8, :].astype(F32)[0:1]
    routed = pieces * lines
    all_ref[routed : routed + half, :] = shared_ref[...].astype(BF)
    gain = gain_ref[...]

    def one_block(block):
        queries = q_ref[block]
        zero = jnp.zeros_like(queries)
        sides = jnp.concatenate(
            [jnp.concatenate([queries, zero], axis=1), jnp.concatenate([zero, queries], axis=1)],
            axis=0,
        )
        lift = lift_ref[block]
        seen = dot(all_ref[...], sides, 1, 0)
        line = lift[MEMS : MEMS + 1]
        near = line * seen[routed:, :width]
        far = line * seen[routed:, width:]
        add = [near, far]
        groups = []
        for part in range(parts):
            for side in range(2):
                total = None
                for one in range(MEMS):
                    start = (one * parts + part) * lines
                    term = lift[one : one + 1] * seen[
                        start : start + lines, side * width : (side + 1) * width
                    ]
                    total = term if total is None else total + term
                groups.append(total)
        combined = local_ref[block] + jnp.concatenate(groups, axis=0) + jnp.concatenate(add, axis=0)
        mean = jnp.sum(combined * combined, axis=0, keepdims=True) * (1.0 / head_size)
        out_ref[block] = (combined * lax.rsqrt(mean + 1e-06) * gain).astype(BF)

    def step(turn, carry):
        one_block(2 * turn)
        one_block(2 * turn + 1)
        return carry

    lax.fori_loop(0, blocks // 2, step, 0)


def shape(dims, dtype):
    return jax.ShapeDtypeStruct(dims, dtype)


def exchange(x, axis):
    return lax.all_to_all(x, axis, split_axis=0, concat_axis=0, tiled=True)


SEND = BF


def spread(keys, values, decay, routes, weights, heads):
    width = keys.shape[0]
    head_size = keys.shape[1] // heads
    args = (keys, values, decay.T, routes.T, weights.T)
    return call(
        fetched(spread_body, len(args)), shape((heads, 2 * head_size + EXTRA, width), BF), *args,
        scratch=held(args), fetch=True,
    )


def turn(queries, heads):
    return call(
        fetched(turn_body, 1), shape((heads, queries.shape[1] // heads, queries.shape[0]), BF),
        queries, scratch=held((queries,)), fetch=True,
    )


def totals(kv, pieces):
    head_size, width = (kv.shape[1] - EXTRA) // 2, kv.shape[2]
    lines = MEMS * head_size // 2 // pieces
    return call(
        functools.partial(totals_body, pieces), shape((pieces, lines + 8, width), SEND), kv,
        scratch=[
            pltpu.VMEM((SETS * head_size, width), F32),
            pltpu.VMEM((kv.shape[0], ROWS, width), F32),
            pltpu.VMEM((SETS * head_size, TOGETHER * 2 * width), BF),
        ],
    )


def prefix(x):
    return call(prefix_body, shape(x.shape, x.dtype), x)


def local(kv, q):
    blocks, head_size, width = q.shape
    return call(
        local_body,
        (shape((blocks, head_size, width), F32), shape((blocks, ROWS, width), F32)),
        kv, q,
        scratch=[
            pltpu.VMEM((SETS * head_size, width), F32),
            pltpu.VMEM((SETS * head_size, width), BF),
            pltpu.VMEM((SETS * head_size, 2 * width), BF),
        ]
        + [pltpu.VMEM((blocks, ROWS, width), F32)] * 5,
    )


def finish(before, q, inner, lift, gain):
    head_size, width = q.shape[1:]
    return call(
        finish_body, shape(q.shape, BF), before, q, inner, lift, gain,
        scratch=[
            pltpu.VMEM((SETS * head_size // 2, width), BF),
            pltpu.VMEM((head_size // 2, width), F32),
        ],
    )


def back(x, tokens, feats):
    return call(back_body, shape((tokens, feats), BF), x)


def on_device(queries, key_vectors, value_vectors, log_decay, routes, route_weight, out_gain):
    heads = lax.axis_size("mem")
    pieces = lax.axis_size("ctx")
    tokens, feats = queries.shape
    head_size = feats // heads
    kv = exchange(spread(key_vectors, value_vectors, log_decay, routes, route_weight, heads), "mem")
    turned = turn(queries, heads)
    q = exchange(turned, "mem")
    group = totals(kv, pieces)
    gathered = exchange(group, "ctx")
    inner, lift = local(kv, q)
    before = exchange(prefix(gathered), "ctx")
    mine = lax.dynamic_slice_in_dim(out_gain, lax.axis_index("mem") * head_size, head_size)
    gain = jnp.broadcast_to(mine[:, None], (head_size, tokens))
    done = exchange(finish(before, q, inner, lift, gain), "mem")
    return back(done, tokens, feats)


def solution(mesh):
    rows = P(("ctx", "mem"), None)

    return jax.shard_map(
        on_device,
        mesh=mesh,
        in_specs=(rows, rows, rows, rows, rows, rows, P()),
        out_specs=rows,
        check_vma=False,
    )
```
